512 devices in a mesh: ctx: 16 (over y, core), head: 4 (over x), dp: 8 (over z).
Axes of the slice: x: 4, y: 8, z: 8, core: 2. Of those that a mesh axis runs over, the one named last changes fastest.
Arguments:
- x_query: bfloat16 [8, 8192, 2560], P('dp', ('ctx', 'head')), may hold values from -6 to 6
- x_key: bfloat16 [8, 8192, 2560], P('dp', ('ctx', 'head')), may hold values from -7 to 7
- values: bfloat16 [8, 8192, 2560], P('dp', ('ctx', 'head')), may hold values from -6 to 6
- grad_out: bfloat16 [8, 8192, 2560], P('dp', ('ctx', 'head')), may hold values from -6 to 6
- gain_query: float32 [2560], replicated, may hold values from 0.5 to 1.5
- gain_key: float32 [2560], replicated, may hold values from 0.5 to 1.5
- key_tiles: int32 [8, 128, 6], P('dp'), may hold values from 0 to 127, as said below
Outputs:
- grad_x_query: bfloat16 [8, 8192, 2560], P('dp', ('ctx', 'head'))
- grad_x_key: bfloat16 [8, 8192, 2560], P('dp', ('ctx', 'head'))
- grad_values: bfloat16 [8, 8192, 2560], P('dp', ('ctx', 'head'))
- grad_gain_query: float32 [2560], replicated
- grad_gain_key: float32 [2560], replicated
The draws below stay inside these ranges and needn't reach their ends.
Inputs may be any that keep to these rules, and one draw needn't show every extreme that they name: `key_tiles`: each row lists 6 distinct tiles. Tiles are grouped in blocks of 8 consecutive tiles; a query tile lists only tiles of its own block and of the blocks just before and after it. The query tiles of one block together list every tile of their own block and exactly 4 distinct tiles of each block beside it.
All inputs are finite; a program needn't handle non-finite values.
Results may differ from the reference program's by a relative error of at most 0.02.
Values may be sent and summed in bfloat16 or wider, within the bound.
No kernel may reach another device: no remote copies, remote signals or barrier semaphores. Data moves between devices by JAX's collectives and lax.ppermute only.
A program may use at most 128 MiB of HBM per device.

```python
import jax
import jax.numpy as jnp
from jax import lax

HEADS = 20
HD = 128
TILE = 64
KSEL = 6
TILE_BLK = 8
W = 2560
NT = 128
S = 8192
B = 8
N_DP = 8


def tile_lists(key):
    blocks = TILE_BLK
    half_blocks = TILE_BLK // 2
    block_count = NT // TILE_BLK

    def one_block(sub_key, block_id):
        first_key, second_key, third_key = jax.random.split(sub_key, 3)
        left_tiles = (block_id - 1) * blocks + jax.random.permutation(first_key, blocks)[:half_blocks]
        right_tiles = (block_id + 1) * blocks + jax.random.permutation(second_key, blocks)[:half_blocks]
        own_tiles = block_id * blocks + jnp.arange(blocks, dtype=jnp.int32)
        candidates = jnp.concatenate([left_tiles.astype(jnp.int32), own_tiles, right_tiles.astype(jnp.int32)])
        present = jnp.concatenate([jnp.full((half_blocks,), block_id > 0), jnp.ones((blocks,), dtype=bool), jnp.full((half_blocks,), block_id < block_count - 1)])
        width_all = blocks + 2 * half_blocks
        ranking = jax.random.permutation(third_key, width_all).astype(jnp.int32) + jnp.where(present, 0, width_all).astype(jnp.int32)
        ordering = jnp.argsort(ranking, stable=True)
        ordered = candidates[ordering]
        total_count = blocks + half_blocks * (block_id > 0).astype(jnp.int32) + half_blocks * (block_id < block_count - 1).astype(jnp.int32)
        positions = (2 * jnp.arange(blocks, dtype=jnp.int32)[:, None] + jnp.arange(KSEL, dtype=jnp.int32)[None, :]) % total_count
        return ordered[positions]
    sub_keys = jax.random.split(jax.random.fold_in(key, 7), B * block_count)
    block_ids = jnp.tile(jnp.arange(block_count, dtype=jnp.int32), B)
    listed = jax.vmap(one_block)(sub_keys, block_ids)
    return listed.reshape(B, NT, KSEL).astype(jnp.int32)


def draw_key_tiles(key, part):
    return tile_lists(key)


def draw_x_query(key, part):
    drawn = jax.random.truncated_normal(jax.random.fold_in(key, 1), -6.0, 6.0, (B, S, W), jnp.float32)
    return drawn.astype(jnp.bfloat16)


def draw_x_key(key, part):
    drawn = jax.random.truncated_normal(jax.random.fold_in(key, 2), -6.0, 6.0, (B, S, W), jnp.float32)
    return drawn.astype(jnp.bfloat16)


def levels(key, extent, cuts, least, high):
    def one(dim, blocks):
        steps = jax.random.uniform(jax.random.fold_in(jax.random.fold_in(key, 6), dim), (blocks,), jnp.float32, least / len(cuts), high / len(cuts))
        return jnp.repeat(jnp.exp(steps), extent[dim] // blocks).reshape((-1,) + (1,) * (len(extent) - dim - 1))

    factor_of = one(*cuts[0])
    for cut in cuts[1:]:
        factor_of = factor_of * one(*cut)
    return factor_of


def centred(stream_key, dims, deviation, bound, cuts=(), held_as=jnp.bfloat16):
    values = jax.random.normal(stream_key, dims, jnp.float32) * deviation
    if len(cuts) > 0:
        values = levels(stream_key, dims, cuts, -0.22, 0.18) * values
    return jnp.clip(values, min=-bound, max=bound).astype(held_as)


def setup_inputs(seed: int = 0) -> dict:
    key_list = jax.random.split(jax.random.key(seed), 8)
    x_query = draw_x_query(jax.random.fold_in(key_list[7], 71), 0)
    x_key = draw_x_key(jax.random.fold_in(key_list[7], 71), 0)
    values = centred(key_list[2], (B, S, W), 1.0, 6.0, ((0, 8), (1, 64)))
    grad_out = centred(key_list[3], (B, S, W), 1.0, 6.0, ((0, 8), (1, 64)))
    gain_query = jnp.clip(1.0 + 0.1 * jax.random.normal(key_list[4], (W,), jnp.float32), 0.5, 1.5)
    gain_key = jnp.clip(1.0 + 0.1 * jax.random.normal(key_list[5], (W,), jnp.float32), 0.5, 1.5)
    key_tiles = draw_key_tiles(jax.random.fold_in(key_list[7], 71), 0)
    return {"x_query": x_query, "x_key": x_key, "values": values, "grad_out": grad_out, "gain_query": gain_query, "gain_key": gain_key, "key_tiles": key_tiles}


epsilon = 1e-06

def normalize(inputs, gain):
    values32 = inputs.astype(jnp.float32)
    scaling = lax.rsqrt(lax.optimization_barrier(jnp.mean(values32 * values32, axis=-1, keepdims=True)) + epsilon)
    return ((values32 * scaling * gain).astype(jnp.bfloat16), scaling)

def unnormalize(inputs, scaling, gain, gradient):
    values32 = inputs.astype(jnp.float32)
    grad32 = gradient.astype(jnp.float32)
    gained = gain * grad32
    result = scaling * gained - values32 * scaling ** 3 * lax.optimization_barrier(jnp.mean(gained * values32, axis=-1, keepdims=True))
    partial_sum = lax.optimization_barrier(jnp.sum((grad32 * values32 * scaling).reshape(-1, inputs.shape[-1]), axis=0))
    return (result.astype(jnp.bfloat16), partial_sum)

def tile_grads(queries, gradient, key_blocks, value_blocks):
    listed = key_blocks.shape
    key_rows = key_blocks.reshape(-1, listed[2], listed[3]).astype(jnp.float32)
    value_rows = value_blocks.reshape(-1, listed[2], listed[3]).astype(jnp.float32)
    query32 = queries.astype(jnp.float32)
    grad32 = gradient.astype(jnp.float32)
    scaling = listed[3] ** (-0.5)
    scores = jnp.einsum('qhd,khd->hqk', query32, key_rows) * scaling
    largest = lax.optimization_barrier(jnp.max(scores, axis=-1, keepdims=True))
    weights = jnp.exp(scores - largest)
    weights = weights / lax.optimization_barrier(jnp.sum(weights, axis=-1, keepdims=True))
    weights_half = weights.astype(jnp.bfloat16)
    attended = jnp.einsum('hqk,khd->qhd', weights_half.astype(jnp.float32), value_rows).astype(jnp.bfloat16)
    row_delta = lax.optimization_barrier(jnp.sum(grad32 * attended.astype(jnp.float32), axis=-1))
    dprob = jnp.einsum('qhd,khd->hqk', grad32, value_rows)
    dscore = (weights * (dprob - jnp.transpose(row_delta)[:, :, None])).astype(jnp.bfloat16)
    dscore32 = dscore.astype(jnp.float32)
    grad_query = (jnp.einsum('hqk,khd->qhd', dscore32, key_rows) * scaling).astype(jnp.bfloat16)
    grad_key = jnp.einsum('hqk,qhd->khd', dscore32, query32) * scaling
    grad_value = jnp.einsum('hqk,qhd->khd', weights_half.astype(jnp.float32), grad32)
    return (grad_query, grad_key.reshape(listed), grad_value.reshape(listed))

def reference(x_query, x_key, values, grad_out, gain_query, gain_key, key_tiles):

    def one_sample(inputs):
        sample_query, sample_key, sample_value, sample_grad, listed_tiles = inputs
        query_norm, scale_query = normalize(sample_query, gain_query)
        key_norm, scale_key = normalize(sample_key, gain_key)
        tile_count = sample_query.shape[0] // TILE
        shape_four = (tile_count, TILE, HEADS, HD)
        query_tiles = query_norm.reshape(shape_four)
        key_blocks = key_norm.reshape(shape_four)
        value_blocks = sample_value.reshape(shape_four)
        grad_tiles = sample_grad.reshape(shape_four)

        def tile_step(carried, step_inputs):
            key_sums, value_sums = carried
            queries, gradient, listed = step_inputs
            grad_query, grad_key, grad_value = tile_grads(queries, gradient, key_blocks[listed], value_blocks[listed])
            return ((key_sums.at[listed].add(grad_key), value_sums.at[listed].add(grad_value)), grad_query)
        empty = jnp.zeros(shape_four, jnp.float32)
        (key_sums, value_sums), query_grads = lax.scan(tile_step, (empty, empty), (query_tiles, grad_tiles, listed_tiles))
        grad_query_rows = query_grads.reshape(sample_query.shape)
        grad_key_rows = key_sums.reshape(sample_query.shape).astype(jnp.bfloat16)
        grad_value_rows = value_sums.reshape(sample_query.shape).astype(jnp.bfloat16)
        query_input_grad, query_part = unnormalize(sample_query, scale_query, gain_query, grad_query_rows)
        key_input_grad, key_part = unnormalize(sample_key, scale_key, gain_key, grad_key_rows)
        return (query_input_grad, key_input_grad, grad_value_rows, query_part, key_part)
    results = lax.map(one_sample, (x_query, x_key, values, grad_out, key_tiles))
    grad_gain_query = lax.optimization_barrier(jnp.sum(results[3], axis=0)) / N_DP
    grad_gain_key = lax.optimization_barrier(jnp.sum(results[4], axis=0)) / N_DP
    return (results[0], results[1], results[2], grad_gain_query, grad_gain_key)
```

```python
import jax
import jax.numpy as jnp
from jax import lax
from jax.experimental import pallas as pl
from jax.experimental.pallas import tpu as pltpu
from jax.sharding import PartitionSpec as P

HD = 128
TILE = 64
ROWS = 16
FAR = -(1 << 20)
GROUP = 4
SIDE = 4

epsilon = 1e-06


def cost(flops, moved, exps=0):
    return pl.CostEstimate(flops=flops, bytes_accessed=moved, transcendentals=exps)


def plan_kernel(listed_ref, plan_ref, slot_ref, *, blocks, listed):
    count = blocks * listed

    def bits(start):
        def step(i, mask):
            tile = listed_ref[start + i]
            inside = jnp.logical_and(tile >= -blocks, tile < 2 * blocks)
            bit = lax.shift_left(jnp.int32(1), jnp.where(inside, tile + blocks, 0))
            return mask | jnp.where(inside, bit, 0)

        return lax.fori_loop(0, count, step, jnp.int32(0))

    before, own, after = bits(0), bits(count), bits(2 * count)
    for i in range(16):
        plan_ref[count + i] = 0
    low, high, to_after, to_before = (jnp.int32(0),) * 4
    for b in range(blocks):
        slot_ref[b] = blocks + low
        slot_ref[blocks + b] = jnp.int32(b)
        slot_ref[2 * blocks + b] = blocks + SIDE + high
        low += lax.shift_right_logical(own, jnp.int32(b)) & 1
        high += lax.shift_right_logical(own, jnp.int32(2 * blocks + b)) & 1
        plan_ref[count + to_after] = jnp.int32(b)
        to_after += lax.shift_right_logical(after, jnp.int32(blocks + b)) & 1
        plan_ref[count + 8 + to_before] = jnp.int32(b)
        to_before += lax.shift_right_logical(before, jnp.int32(blocks + b)) & 1

    def place(i, carry):
        tile = jnp.clip(listed_ref[count + i], -blocks, 2 * blocks - 1)
        plan_ref[i] = slot_ref[tile + blocks]
        return carry

    lax.fori_loop(0, count, place, jnp.int32(0))


def make_plan(key_tiles, blocks):
    listed = key_tiles.shape[2]
    start = lax.axis_index("ctx") * blocks
    padded = jnp.pad(key_tiles[0] - start, ((blocks, blocks), (0, 0)), constant_values=FAR)
    near = lax.dynamic_slice_in_dim(padded, start, 3 * blocks, 0).reshape(-1)
    count = blocks * listed
    return pl.pallas_call(
        lambda a, b, c: plan_kernel(a, b, c, blocks=blocks, listed=listed),
        out_shape=jax.ShapeDtypeStruct((count + 16,), jnp.int32),
        in_specs=[pl.BlockSpec(memory_space=pltpu.SMEM)],
        out_specs=pl.BlockSpec(memory_space=pltpu.SMEM),
        scratch_shapes=[pltpu.SMEM((3 * blocks,), jnp.int32)],
        cost_estimate=cost(1000, 1000),
        name="plan",
    )(near)


def norm_kernel(x_ref, y_ref, gain_ref, out_ref, *, groups, heads):
    width = groups * heads * HD

    def step(c, carry):
        rows = pl.ds(c * ROWS, ROWS)
        x = x_ref[rows, :].astype(jnp.float32)
        scaling = lax.rsqrt(jnp.sum(x * x, axis=-1, keepdims=True) / width + epsilon)
        for g in range(groups):
            for h in range(heads):
                cols = slice((g * heads + h) * HD, (g * heads + h + 1) * HD)
                part = x_ref[rows, cols].astype(jnp.float32) * scaling * gain_ref[:, cols]
                out_ref[g, 0, h, 0, rows, :] = part.astype(jnp.bfloat16)
                out_ref[g, 1, h, 0, rows, :] = y_ref[rows, cols]
        return carry

    lax.fori_loop(0, TILE // ROWS, step, 0)


def norm_pack(x, y, gain, groups, name):
    tokens, width = x.shape
    heads = width // HD // groups
    tiles = tokens // TILE
    return pl.pallas_call(
        lambda *refs: norm_kernel(*refs, groups=groups, heads=heads),
        grid=(tiles,),
        out_shape=jax.ShapeDtypeStruct((groups, 2, heads, tiles, TILE, HD), jnp.bfloat16),
        in_specs=[
            pl.BlockSpec((TILE, width), lambda i: (i, 0)),
            pl.BlockSpec((TILE, width), lambda i: (i, 0)),
            pl.BlockSpec((1, width), lambda i: (0, 0)),
        ],
        out_specs=pl.BlockSpec(
            (groups, 2, heads, 1, TILE, HD), lambda i: (0, 0, 0, i, 0, 0)
        ),
        cost_estimate=cost(8 * tokens * width, 8 * tokens * width),
        name=name,
    )(x, y, gain.reshape(1, width))


def unnorm_kernel(x_ref, back_ref, gain_ref, out_ref, *rest, groups, heads):
    width = groups * heads * HD
    pair = len(back_ref.shape) == 6

    def step(c, carry):
        rows = pl.ds(c * ROWS, ROWS)
        x = x_ref[rows, :].astype(jnp.float32)
        square = jnp.sum(x * x, axis=-1, keepdims=True) / width
        scaling = lax.rsqrt(square + epsilon)
        total = jnp.zeros((ROWS, HD), jnp.float32)
        for g in range(groups):
            for h in range(heads):
                cols = slice((g * heads + h) * HD, (g * heads + h + 1) * HD)
                grad = back_ref[g, 0, h, 0, rows, :] if pair else back_ref[g, h, 0, rows, :]
                gained = grad.astype(jnp.float32) * gain_ref[:, cols]
                total += gained * x_ref[rows, cols].astype(jnp.float32)
        mean = jnp.sum(total, axis=-1, keepdims=True) / width
        factor = scaling * scaling * scaling * mean
        for g in range(groups):
            for h in range(heads):
                cols = slice((g * heads + h) * HD, (g * heads + h + 1) * HD)
                grad = back_ref[g, 0, h, 0, rows, :] if pair else back_ref[g, h, 0, rows, :]
                gained = grad.astype(jnp.float32) * gain_ref[:, cols]
                part = scaling * gained - x_ref[rows, cols].astype(jnp.float32) * factor
                out_ref[rows, cols] = part.astype(jnp.bfloat16)
                if pair:
                    rest[0][rows, cols] = back_ref[g, 1, h, 0, rows, :]
        return carry

    lax.fori_loop(0, TILE // ROWS, step, 0)


def unnorm(x, back, gain, name):
    tokens, width = x.shape
    groups = back.shape[0]
    heads = width // HD // groups
    pair = back.ndim == 6
    outs = 2 if pair else 1
    back_block = (groups, 2, heads, 1, TILE, HD) if pair else (groups, heads, 1, TILE, HD)
    back_map = (lambda i: (0, 0, 0, i, 0, 0)) if pair else (lambda i: (0, 0, i, 0, 0))
    return pl.pallas_call(
        lambda *refs: unnorm_kernel(*refs, groups=groups, heads=heads),
        grid=(tokens // TILE,),
        out_shape=[jax.ShapeDtypeStruct((tokens, width), jnp.bfloat16)] * outs,
        in_specs=[
            pl.BlockSpec((TILE, width), lambda i: (i, 0)),
            pl.BlockSpec(back_block, back_map),
            pl.BlockSpec((1, width), lambda i: (0, 0)),
        ],
        out_specs=[pl.BlockSpec((TILE, width), lambda i: (i, 0))] * outs,
        cost_estimate=cost(12 * tokens * width, 8 * tokens * width),
        name=name,
    )(x, back, gain.reshape(1, width))


def pack_kernel(plan_ref, kv_ref, after_ref, before_ref, *, count):
    for which, out_ref in ((0, after_ref), (8, before_ref)):
        for r in range(SIDE):
            tile = plan_ref[count + which + r]
            for kv in range(2):
                out_ref[kv, 0, r] = kv_ref[tile // 2, kv, 0, tile % 2]


def pack(plan, kv, count):
    groups, _, heads, tiles, _, _ = kv.shape
    side = jax.ShapeDtypeStruct((2, heads, SIDE, TILE, HD), kv.dtype)
    side_spec = pl.BlockSpec((2, 1, SIDE, TILE, HD), lambda h: (0, h, 0, 0, 0))
    return pl.pallas_call(
        lambda *refs: pack_kernel(*refs, count=count),
        grid=(heads,),
        out_shape=[side, side],
        in_specs=[
            pl.BlockSpec(memory_space=pltpu.SMEM),
            pl.BlockSpec((groups, 2, 1, tiles, TILE, HD), lambda h: (0, 0, h, 0, 0, 0)),
        ],
        out_specs=[side_spec, side_spec],
        cost_estimate=cost(1000, 4 * kv.size),
        name="pack",
    )(plan, kv)


def merge_kernel(plan_ref, own_ref, after_ref, before_ref, out_ref, total_ref, *, count):
    total_ref[...] = own_ref[...]
    for which, side_ref in ((0, after_ref), (8, before_ref)):
        for r in range(SIDE):
            tile = plan_ref[count + which + r]
            for kv in range(2):
                total_ref[tile // 2, kv, 0, tile % 2] += side_ref[kv, 0, r].astype(jnp.float32)
    out_ref[...] = total_ref[...].astype(jnp.bfloat16)


def merge(plan, own, after, before, count):
    groups, _, heads, tiles, _, _ = own.shape
    side_spec = pl.BlockSpec((2, 1, SIDE, TILE, HD), lambda h: (0, h, 0, 0, 0))
    block = pl.BlockSpec((groups, 2, 1, tiles, TILE, HD), lambda h: (0, 0, h, 0, 0, 0))
    return pl.pallas_call(
        lambda *refs: merge_kernel(*refs, count=count),
        grid=(heads,),
        out_shape=jax.ShapeDtypeStruct(own.shape, jnp.bfloat16),
        in_specs=[pl.BlockSpec(memory_space=pltpu.SMEM), block, side_spec, side_spec],
        out_specs=block,
        scratch_shapes=[pltpu.VMEM((groups, 2, 1, tiles, TILE, HD), jnp.float32)],
        cost_estimate=cost(own.size, 6 * own.size),
        name="merge",
    )(plan, own, after, before)


def dot(a, b, dims):
    return lax.dot_general(a, b, (dims, ((), ())), preferred_element_type=jnp.float32)


def attend_kernel(
    plan_ref,
    qd_ref,
    kv_ref,
    low_ref,
    high_ref,
    dq_ref,
    own_ref,
    to_low_ref,
    to_high_ref,
    gain_ref,
    keys_ref,
    values_ref,
    dk_ref,
    dv_ref,
    *,
    blocks,
    listed,
):
    scaling = HD**-0.5
    slots = blocks + 2 * SIDE
    for b in range(blocks):
        keys_ref[b] = kv_ref[b // 2, 0, 0, b % 2]
        values_ref[b] = kv_ref[b // 2, 1, 0, b % 2]
    for r in range(SIDE):
        keys_ref[blocks + r] = low_ref[0, 0, r]
        values_ref[blocks + r] = low_ref[1, 0, r]
        keys_ref[blocks + SIDE + r] = high_ref[0, 0, r]
        values_ref[blocks + SIDE + r] = high_ref[1, 0, r]
    dk_ref[...] = jnp.zeros_like(dk_ref)
    dv_ref[...] = jnp.zeros_like(dv_ref)

    def together(first, gain_sum):
        tiles = range(GROUP)
        at = [[plan_ref[(first + t) * listed + j] for j in range(listed)] for t in tiles]
        where = [((first + t) // 2, (first + t) % 2) for t in tiles]
        queries = [qd_ref[source, 0, 0, half] for source, half in where]
        gradient = [qd_ref[source, 1, 0, half] for source, half in where]
        keys = [jnp.concatenate([keys_ref[a] for a in at[t]], axis=0) for t in tiles]
        vals = [jnp.concatenate([values_ref[a] for a in at[t]], axis=0) for t in tiles]
        scores = [dot(keys[t], queries[t], ((1,), (1,))) for t in tiles]
        dprob = [dot(vals[t], gradient[t], ((1,), (1,))) for t in tiles]
        largest = [jnp.max(x, axis=0, keepdims=True) for x in scores]
        powers = [jnp.exp((scores[t] - largest[t]) * scaling) for t in tiles]
        inverse = [1.0 / jnp.sum(x, axis=0, keepdims=True) for x in powers]
        weights = [powers[t] * inverse[t] for t in tiles]
        rounded = [x.astype(jnp.bfloat16) for x in weights]
        grad_value = [dot(rounded[t], gradient[t], ((1,), (0,))) for t in tiles]
        delta = [
            jnp.sum(rounded[t].astype(jnp.float32) * dprob[t], axis=0, keepdims=True)
            for t in tiles
        ]
        dscore = [(weights[t] * (dprob[t] - delta[t])).astype(jnp.bfloat16) for t in tiles]
        grad_key = [dot(dscore[t], queries[t], ((1,), (0,))) for t in tiles]
        grad_query = [
            (dot(dscore[t], keys[t], ((0,), (0,))) * scaling).astype(jnp.bfloat16) for t in tiles
        ]
        for t in tiles:
            dq_ref[where[t][0], 0, where[t][1]] = grad_query[t]
            product = grad_query[t].astype(jnp.float32) * queries[t].astype(jnp.float32)
            gain_sum += jnp.sum(product.reshape(-1, 8, HD), axis=0)
            for j, a in enumerate(at[t]):
                dk_ref[a] += grad_key[t][j * TILE : (j + 1) * TILE]
                dv_ref[a] += grad_value[t][j * TILE : (j + 1) * TILE]
        return gain_sum

    gain_query = jnp.zeros((8, HD), jnp.float32)
    for first in range(0, blocks, GROUP):
        gain_query = together(first, gain_query)
    gain_key = jnp.zeros((8, HD), jnp.float32)
    for s in range(slots):
        grad_key = dk_ref[s] * scaling
        gain_key += jnp.sum(
            (grad_key * keys_ref[s].astype(jnp.float32)).reshape(-1, 8, HD), axis=0
        )
        if s < blocks:
            own_ref[s // 2, 0, 0, s % 2] = grad_key
            own_ref[s // 2, 1, 0, s % 2] = dv_ref[s]
        else:
            out_ref = to_low_ref if s < blocks + SIDE else to_high_ref
            r = (s - blocks) % SIDE
            out_ref[0, 0, r] = grad_key.astype(jnp.bfloat16)
            out_ref[1, 0, r] = dv_ref[s].astype(jnp.bfloat16)
    gain_ref[0, 0:1] = jnp.sum(gain_query, axis=0, keepdims=True)
    gain_ref[0, 1:2] = jnp.sum(gain_key, axis=0, keepdims=True)


def attend(plan, qd, kv, low, high, blocks, listed):
    groups, _, heads, tiles, _, _ = kv.shape
    slots = blocks + 2 * SIDE
    side = jax.ShapeDtypeStruct(low.shape, jnp.bfloat16)
    side_spec = pl.BlockSpec((2, 1, SIDE, TILE, HD), lambda h: (0, h, 0, 0, 0))
    block = pl.BlockSpec((groups, 2, 1, tiles, TILE, HD), lambda h: (0, 0, h, 0, 0, 0))
    work = heads * blocks * TILE * listed * TILE
    return pl.pallas_call(
        lambda *refs: attend_kernel(*refs, blocks=blocks, listed=listed),
        grid=(heads,),
        out_shape=[
            jax.ShapeDtypeStruct((groups, heads, tiles, TILE, HD), jnp.bfloat16),
            jax.ShapeDtypeStruct(kv.shape, jnp.float32),
            side,
            side,
            jax.ShapeDtypeStruct((heads, 2, HD), jnp.float32),
        ],
        in_specs=[pl.BlockSpec(memory_space=pltpu.SMEM), block, block, side_spec, side_spec],
        out_specs=[
            pl.BlockSpec((groups, 1, tiles, TILE, HD), lambda h: (0, h, 0, 0, 0)),
            block,
            side_spec,
            side_spec,
            pl.BlockSpec((1, 2, HD), lambda h: (h, 0, 0)),
        ],
        scratch_shapes=[
            pltpu.VMEM((slots, TILE, HD), jnp.bfloat16),
            pltpu.VMEM((slots, TILE, HD), jnp.bfloat16),
            pltpu.VMEM((slots, TILE, HD), jnp.float32),
            pltpu.VMEM((slots, TILE, HD), jnp.float32),
        ],
        cost_estimate=cost(12 * work * HD, 20 * kv.size, work),
        name="attend",
    )(plan, qd, kv, low, high)


def swap(block):
    return lax.all_to_all(block, "head", split_axis=0, concat_axis=0, tiled=True)


def shift(block, distance):
    devices = range(lax.axis_size("ctx"))
    route = [(i - distance, i) for i in devices if i - distance in devices]
    return lax.ppermute(block, "ctx", route)


def gathered(block, axis):
    count = lax.axis_size(axis)
    copies = jnp.broadcast_to(block[None], (count,) + block.shape)
    return lax.all_to_all(copies, axis, split_axis=0, concat_axis=0, tiled=True)


def per_device(x_query, x_key, values, grad_out, gain_query, gain_key, key_tiles):
    groups = lax.axis_size("head")
    blocks = groups * x_query.shape[1] // TILE
    listed = key_tiles.shape[2]
    count = blocks * listed
    kv = swap(norm_pack(x_key[0], values[0], gain_key, groups, "norm_key"))
    plan = make_plan(key_tiles, blocks)
    qd = swap(norm_pack(x_query[0], grad_out[0], gain_query, groups, "norm_query"))
    after, before = pack(plan, kv, count)
    low, high = shift(after, 1), shift(before, -1)
    dq, own, to_low, to_high, gains = attend(plan, qd, kv, low, high, blocks, listed)
    back_query = swap(dq)
    from_after, from_before = shift(to_low, -1), shift(to_high, 1)
    merged = merge(plan, own, from_after, from_before, count)
    back = swap(merged)
    (grad_x_query,) = unnorm(x_query[0], back_query, gain_query, "unnorm_query")
    grad_x_key, grad_values = unnorm(x_key[0], back, gain_key, "unnorm_key")
    gains = jnp.sum(gathered(gains, "dp"), axis=0)
    gains = jnp.sum(gathered(gains, "ctx"), axis=0)
    gains = gathered(gains, "head").transpose(2, 0, 1, 3).reshape(2, -1)
    samples = lax.axis_size("dp")
    return (
        grad_x_query[None],
        grad_x_key[None],
        grad_values[None],
        gains[0] / gain_query / samples,
        gains[1] / gain_key / samples,
    )


def solution(mesh):
    placed = P("dp", ("ctx", "head"), None)
    return jax.shard_map(
        per_device,
        mesh=mesh,
        in_specs=(placed, placed, placed, placed, P(), P(), P("dp", None, None)),
        out_specs=(placed, placed, placed, P(), P()),
        check_vma=False,
    )
```

```python
import jax
import jax.numpy as jnp
from jax import lax
from jax.experimental import pallas as pl
from jax.experimental.pallas import tpu as pltpu
from jax.sharding import PartitionSpec as P

HD = 128
TILE = 64
ROWS = 16
FAR = -(1 << 20)
GROUP = 4
SIDE = 4

epsilon = 1e-06


def cost(flops, moved, exps=0):
    return pl.CostEstimate(flops=flops, bytes_accessed=moved, transcendentals=exps)


def room(mebibytes):
    return pltpu.CompilerParams(vmem_limit_bytes=mebibytes << 20)


def in_hbm(block):
    return pltpu.with_memory_space_constraint(block, pltpu.HBM)


def plan_kernel(listed_ref, plan_ref, slot_ref, *, blocks, listed):
    count = blocks * listed

    def bits(start):
        def step(i, mask):
            tile = listed_ref[start + i]
            inside = jnp.logical_and(tile >= -blocks, tile < 2 * blocks)
            bit = lax.shift_left(jnp.int32(1), jnp.where(inside, tile + blocks, 0))
            return mask | jnp.where(inside, bit, 0)

        return lax.fori_loop(0, count, step, jnp.int32(0))

    before, own, after = bits(0), bits(count), bits(2 * count)
    for i in range(16):
        plan_ref[count + i] = 0
    low, high, to_after, to_before = (jnp.int32(0),) * 4
    for b in range(blocks):
        slot_ref[b] = blocks + low
        slot_ref[blocks + b] = jnp.int32(b)
        slot_ref[2 * blocks + b] = blocks + SIDE + high
        low += lax.shift_right_logical(own, jnp.int32(b)) & 1
        high += lax.shift_right_logical(own, jnp.int32(2 * blocks + b)) & 1
        plan_ref[count + to_after] = jnp.int32(b)
        to_after += lax.shift_right_logical(after, jnp.int32(blocks + b)) & 1
        plan_ref[count + 8 + to_before] = jnp.int32(b)
        to_before += lax.shift_right_logical(before, jnp.int32(blocks + b)) & 1

    def place(i, carry):
        tile = jnp.clip(listed_ref[count + i], -blocks, 2 * blocks - 1)
        plan_ref[i] = slot_ref[tile + blocks]
        return carry

    lax.fori_loop(0, count, place, jnp.int32(0))


def make_plan(key_tiles, blocks):
    listed = key_tiles.shape[2]
    start = lax.axis_index("ctx") * blocks
    padded = jnp.pad(key_tiles[0] - start, ((blocks, blocks), (0, 0)), constant_values=FAR)
    near = lax.dynamic_slice_in_dim(padded, start, 3 * blocks, 0).reshape(-1)
    count = blocks * listed
    return pl.pallas_call(
        lambda a, b, c: plan_kernel(a, b, c, blocks=blocks, listed=listed),
        out_shape=jax.ShapeDtypeStruct((count + 16,), jnp.int32),
        in_specs=[pl.BlockSpec(memory_space=pltpu.SMEM)],
        out_specs=pl.BlockSpec(memory_space=pltpu.SMEM),
        scratch_shapes=[pltpu.SMEM((3 * blocks,), jnp.int32)],
        cost_estimate=cost(1000, 1000),
        name="plan",
    )(near)


def norm_kernel(x_ref, y_ref, gain_ref, out_ref, *, groups, heads):
    width = groups * heads * HD

    def step(c, carry):
        rows = pl.ds(c * ROWS, ROWS)
        x = x_ref[rows, :].astype(jnp.float32)
        scaling = lax.rsqrt(jnp.sum(x * x, axis=-1, keepdims=True) / width + epsilon)
        for g in range(groups):
            for h in range(heads):
                cols = slice((g * heads + h) * HD, (g * heads + h + 1) * HD)
                part = x_ref[rows, cols].astype(jnp.float32) * scaling * gain_ref[cols][None, :]
                out_ref[g, 0, h, 0, rows, :] = part.astype(jnp.bfloat16)
                out_ref[g, 1, h, 0, rows, :] = y_ref[rows, cols]
        return carry

    lax.fori_loop(0, TILE // ROWS, step, 0)


def norm_pack(x, y, gain, groups, name, grant):
    tokens, width = x.shape
    heads = width // HD // groups
    tiles = tokens // TILE
    return pl.pallas_call(
        lambda *refs: norm_kernel(*refs, groups=groups, heads=heads),
        grid=(tiles,),
        out_shape=jax.ShapeDtypeStruct((groups, 2, heads, tiles, TILE, HD), jnp.bfloat16),
        in_specs=[
            pl.BlockSpec((TILE, width), lambda i: (i, 0)),
            pl.BlockSpec((TILE, width), lambda i: (i, 0)),
            pl.BlockSpec((width,), lambda i: (0,)),
        ],
        out_specs=pl.BlockSpec(
            (groups, 2, heads, 1, TILE, HD), lambda i: (0, 0, 0, i, 0, 0)
        ),
        compiler_params=room(grant),
        cost_estimate=cost(8 * tokens * width, 8 * tokens * width),
        name=name,
    )(x, y, gain)


def unnorm_kernel(xq_ref, xk_ref, back_ref, gq_ref, gk_ref, oq_ref, ok_ref, ov_ref, *, groups, heads):
    width = groups * heads * HD
    places = [(g, h, slice((g * heads + h) * HD, (g * heads + h + 1) * HD)) for g in range(groups) for h in range(heads)]

    def step(c, carry):
        rows = pl.ds(c * ROWS, ROWS)
        for which, x_ref, gain_ref, out_ref in ((0, xq_ref, gq_ref, oq_ref), (1, xk_ref, gk_ref, ok_ref)):
            square = jnp.zeros((ROWS, HD), jnp.float32)
            total = jnp.zeros((ROWS, HD), jnp.float32)
            for g, h, cols in places:
                x = x_ref[rows, cols].astype(jnp.float32)
                gained = back_ref[g, which, h, 0, rows, :].astype(jnp.float32) * gain_ref[cols][None, :]
                square += x * x
                total += gained * x
            scaling = lax.rsqrt(jnp.sum(square, axis=-1, keepdims=True) / width + epsilon)
            mean = jnp.sum(total, axis=-1, keepdims=True) / width
            factor = scaling * scaling * scaling * mean
            for g, h, cols in places:
                x = x_ref[rows, cols].astype(jnp.float32)
                gained = back_ref[g, which, h, 0, rows, :].astype(jnp.float32) * gain_ref[cols][None, :]
                out_ref[rows, cols] = (scaling * gained - x * factor).astype(jnp.bfloat16)
                if which:
                    ov_ref[rows, cols] = back_ref[g, 2, h, 0, rows, :]
        return carry

    lax.fori_loop(0, TILE // ROWS, step, 0)


def unnorm(xq, xk, back, gain_query, gain_key):
    tokens, width = xq.shape
    groups, _, heads = back.shape[:3]
    rows = pl.BlockSpec((TILE, width), lambda i: (i, 0))
    gain = pl.BlockSpec((width,), lambda i: (0,))
    return pl.pallas_call(
        lambda *refs: unnorm_kernel(*refs, groups=groups, heads=heads),
        grid=(tokens // TILE,),
        out_shape=[jax.ShapeDtypeStruct((tokens, width), jnp.bfloat16)] * 3,
        in_specs=[
            rows,
            rows,
            pl.BlockSpec((groups, 3, heads, 1, TILE, HD), lambda i: (0, 0, 0, i, 0, 0)),
            gain,
            gain,
        ],
        out_specs=[rows] * 3,
        compiler_params=room(16),
        cost_estimate=cost(24 * tokens * width, 16 * tokens * width),
        name="unnorm",
    )(xq, xk, back, gain_query, gain_key)


def pack_kernel(plan_ref, kv_ref, after_ref, before_ref, *, count):
    for which, out_ref in ((0, after_ref), (8, before_ref)):
        for r in range(SIDE):
            tile = plan_ref[count + which + r]
            for kv in range(2):
                out_ref[kv, 0, r] = kv_ref[tile // 2, kv, 0, tile % 2]


def pack(plan, kv, count):
    groups, _, heads, tiles, _, _ = kv.shape
    side = jax.ShapeDtypeStruct((2, heads, SIDE, TILE, HD), kv.dtype)
    side_spec = pl.BlockSpec((2, 1, SIDE, TILE, HD), lambda h: (0, h, 0, 0, 0))
    return pl.pallas_call(
        lambda *refs: pack_kernel(*refs, count=count),
        grid=(heads,),
        out_shape=[side, side],
        in_specs=[
            pl.BlockSpec(memory_space=pltpu.SMEM),
            pl.BlockSpec((groups, 2, 1, tiles, TILE, HD), lambda h: (0, 0, h, 0, 0, 0)),
        ],
        out_specs=[side_spec, side_spec],
        compiler_params=room(8),
        cost_estimate=cost(1000, 4 * kv.size),
        name="pack",
    )(plan, kv)


def merge_kernel(plan_ref, dq_ref, own_ref, after_ref, before_ref, out_ref, total_ref, *, count):
    total_ref[...] = own_ref[:, :, 0].astype(jnp.float32)
    for which, side_ref in ((0, after_ref), (8, before_ref)):
        for r in range(SIDE):
            tile = plan_ref[count + which + r]
            for kv in range(2):
                total_ref[tile // 2, kv, tile % 2] += side_ref[kv, 0, r].astype(jnp.float32)
    out_ref[:, 0, 0] = dq_ref[:, 0]
    out_ref[:, 1:, 0] = total_ref[...].astype(jnp.bfloat16)


def merge(plan, dq, own, after, before, count):
    groups, _, heads, tiles, _, _ = own.shape
    side_spec = pl.BlockSpec((2, 1, SIDE, TILE, HD), lambda h: (0, h, 0, 0, 0))
    return pl.pallas_call(
        lambda *refs: merge_kernel(*refs, count=count),
        grid=(heads,),
        out_shape=jax.ShapeDtypeStruct((groups, 3, heads, tiles, TILE, HD), jnp.bfloat16),
        in_specs=[
            pl.BlockSpec(memory_space=pltpu.SMEM),
            pl.BlockSpec((groups, 1, tiles, TILE, HD), lambda h: (0, h, 0, 0, 0)),
            pl.BlockSpec((groups, 2, 1, tiles, TILE, HD), lambda h: (0, 0, h, 0, 0, 0)),
            side_spec,
            side_spec,
        ],
        out_specs=pl.BlockSpec((groups, 3, 1, tiles, TILE, HD), lambda h: (0, 0, h, 0, 0, 0)),
        scratch_shapes=[pltpu.VMEM((groups, 2, tiles, TILE, HD), jnp.float32)],
        compiler_params=room(8),
        cost_estimate=cost(own.size, 6 * own.size),
        name="merge",
    )(plan, dq, own, after, before)


def dot(a, b, dims):
    return lax.dot_general(a, b, (dims, ((), ())), preferred_element_type=jnp.float32)


def attend_kernel(
    plan_ref,
    qd_ref,
    kv_ref,
    low_ref,
    high_ref,
    dq_ref,
    own_ref,
    to_low_ref,
    to_high_ref,
    gain_ref,
    keys_ref,
    values_ref,
    dk_ref,
    dv_ref,
    *,
    blocks,
    listed,
):
    scaling = HD**-0.5
    slots = blocks + 2 * SIDE
    for b in range(blocks):
        keys_ref[b] = kv_ref[b // 2, 0, 0, b % 2]
        values_ref[b] = kv_ref[b // 2, 1, 0, b % 2]
    for r in range(SIDE):
        keys_ref[blocks + r] = low_ref[0, 0, r]
        values_ref[blocks + r] = low_ref[1, 0, r]
        keys_ref[blocks + SIDE + r] = high_ref[0, 0, r]
        values_ref[blocks + SIDE + r] = high_ref[1, 0, r]

    @pl.when(pl.program_id(0) == 0)
    def _():
        gain_ref[...] = jnp.zeros_like(gain_ref)

    dk_ref[...] = jnp.zeros_like(dk_ref)
    dv_ref[...] = jnp.zeros_like(dv_ref)

    def together(first, gain_sum):
        tiles = range(GROUP)
        at = [[plan_ref[(first + t) * listed + j] for j in range(listed)] for t in tiles]
        where = [((first + t) // 2, (first + t) % 2) for t in tiles]
        queries = [qd_ref[source, 0, 0, half] for source, half in where]
        gradient = [qd_ref[source, 1, 0, half] for source, half in where]
        keys = [jnp.concatenate([keys_ref[a] for a in at[t]], axis=0) for t in tiles]
        vals = [jnp.concatenate([values_ref[a] for a in at[t]], axis=0) for t in tiles]
        scores = [dot(keys[t], queries[t], ((1,), (1,))) for t in tiles]
        dprob = [dot(vals[t], gradient[t], ((1,), (1,))) for t in tiles]
        largest = [jnp.max(x, axis=0, keepdims=True) for x in scores]
        powers = [jnp.exp((scores[t] - largest[t]) * scaling) for t in tiles]
        inverse = [1.0 / jnp.sum(x, axis=0, keepdims=True) for x in powers]
        weights = [powers[t] * inverse[t] for t in tiles]
        rounded = [x.astype(jnp.bfloat16) for x in weights]
        grad_value = [dot(rounded[t], gradient[t], ((1,), (0,))) for t in tiles]
        delta = [
            jnp.sum(rounded[t].astype(jnp.float32) * dprob[t], axis=0, keepdims=True)
            for t in tiles
        ]
        dscore = [(weights[t] * (dprob[t] - delta[t])).astype(jnp.bfloat16) for t in tiles]
        grad_key = [dot(dscore[t], queries[t], ((1,), (0,))) for t in tiles]
        grad_query = [
            (dot(dscore[t], keys[t], ((0,), (0,))) * scaling).astype(jnp.bfloat16) for t in tiles
        ]
        for t in tiles:
            dq_ref[where[t][0], 0, where[t][1]] = grad_query[t]
            product = grad_query[t].astype(jnp.float32) * queries[t].astype(jnp.float32)
            gain_sum += jnp.sum(product.reshape(-1, 8, HD), axis=0)
            for j, a in enumerate(at[t]):
                dk_ref[a] += grad_key[t][j * TILE : (j + 1) * TILE]
                dv_ref[a] += grad_value[t][j * TILE : (j + 1) * TILE]
        return gain_sum

    gain_query = jnp.zeros((8, HD), jnp.float32)
    for first in range(0, blocks, GROUP):
        gain_query = together(first, gain_query)
    gain_key = jnp.zeros((8, HD), jnp.float32)
    for s in range(slots):
        grad_key = dk_ref[s] * scaling
        gain_key += jnp.sum(
            (grad_key * keys_ref[s].astype(jnp.float32)).reshape(-1, 8, HD), axis=0
        )
        if s < blocks:
            own_ref[s // 2, 0, 0, s % 2] = grad_key.astype(jnp.bfloat16)
            own_ref[s // 2, 1, 0, s % 2] = dv_ref[s].astype(jnp.bfloat16)
        else:
            out_ref = to_low_ref if s < blocks + SIDE else to_high_ref
            r = (s - blocks) % SIDE
            out_ref[0, 0, r] = grad_key.astype(jnp.bfloat16)
            out_ref[1, 0, r] = dv_ref[s].astype(jnp.bfloat16)
    head = pl.program_id(0)
    for which, part in ((0, gain_query), (8, gain_key)):
        gain_ref[pl.ds(which + head, 1)] = jnp.sum(part, axis=0, keepdims=True)


def attend(plan, qd, kv, low, high, blocks, listed):
    groups, _, heads, tiles, _, _ = kv.shape
    slots = blocks + 2 * SIDE
    side = jax.ShapeDtypeStruct(low.shape, jnp.bfloat16)
    side_spec = pl.BlockSpec((2, 1, SIDE, TILE, HD), lambda h: (0, h, 0, 0, 0))
    block = pl.BlockSpec((groups, 2, 1, tiles, TILE, HD), lambda h: (0, 0, h, 0, 0, 0))
    work = heads * blocks * TILE * listed * TILE
    return pl.pallas_call(
        lambda *refs: attend_kernel(*refs, blocks=blocks, listed=listed),
        grid=(heads,),
        out_shape=[
            jax.ShapeDtypeStruct((groups, heads, tiles, TILE, HD), jnp.bfloat16),
            pltpu.HBM(kv.shape, jnp.bfloat16),
            side,
            side,
            jax.ShapeDtypeStruct((16, HD), jnp.float32),
        ],
        in_specs=[pl.BlockSpec(memory_space=pltpu.SMEM), block, block, side_spec, side_spec],
        out_specs=[
            pl.BlockSpec((groups, 1, tiles, TILE, HD), lambda h: (0, h, 0, 0, 0)),
            block,
            side_spec,
            side_spec,
            pl.BlockSpec((16, HD), lambda h: (0, 0)),
        ],
        scratch_shapes=[
            pltpu.VMEM((slots, TILE, HD), jnp.bfloat16),
            pltpu.VMEM((slots, TILE, HD), jnp.bfloat16),
            pltpu.VMEM((slots, TILE, HD), jnp.float32),
            pltpu.VMEM((slots, TILE, HD), jnp.float32),
        ],
        compiler_params=room(24),
        cost_estimate=cost(12 * work * HD, 20 * kv.size, work),
        name="attend",
    )(plan, qd, kv, low, high)


def swap(block):
    return lax.all_to_all(block, "head", split_axis=0, concat_axis=0, tiled=True)


def shift(block, distance):
    devices = range(lax.axis_size("ctx"))
    route = [(i - distance, i) for i in devices if i - distance in devices]
    return lax.ppermute(block, "ctx", route)


def gathered(block, axis):
    count = lax.axis_size(axis)
    copies = jnp.broadcast_to(block[None], (count,) + block.shape)
    return lax.all_to_all(copies, axis, split_axis=0, concat_axis=0, tiled=True)


def per_device(x_query, x_key, values, grad_out, gain_query, gain_key, key_tiles):
    groups = lax.axis_size("head")
    blocks = groups * x_query.shape[1] // TILE
    listed = key_tiles.shape[2]
    count = blocks * listed
    kv = swap(norm_pack(x_key[0], values[0], gain_key, groups, "norm_key", 60))
    plan, gain = lax.optimization_barrier((make_plan(key_tiles, blocks), gain_query))
    qd = swap(norm_pack(x_query[0], grad_out[0], gain, groups, "norm_query", 16))
    after, before = pack(plan, kv, count)
    low, high = (in_hbm(side) for side in (shift(after, 1), shift(before, -1)))
    dq, own, to_low, to_high, gains = attend(plan, qd, kv, low, high, blocks, listed)
    from_after, from_before = shift(to_low, -1), shift(to_high, 1)
    gains = jnp.sum(gathered(gains, "dp"), axis=0)
    from_after, from_before, gains = lax.optimization_barrier((from_after, from_before, gains))
    merged = merge(plan, dq, own, from_after, from_before, count)
    merged, gains = lax.optimization_barrier((merged, gains))
    back = swap(merged)
    gains = jnp.sum(lax.all_gather(gains, "ctx"), axis=0)
    gains = lax.all_gather(gains, "head")
    grad_x_query, grad_x_key, grad_values = unnorm(
        x_query[0], x_key[0], back, gain_query, gain_key
    )
    heads = x_query.shape[2] // HD // groups
    gains = [gains[:, at : at + heads].reshape(-1) for at in (0, 8)]
    samples = lax.axis_size("dp")
    return (
        grad_x_query[None],
        grad_x_key[None],
        grad_values[None],
        gains[0] / gain_query / samples,
        gains[1] / gain_key / samples,
    )


def solution(mesh):
    placed = P("dp", ("ctx", "head"), None)
    return jax.shard_map(
        per_device,
        mesh=mesh,
        in_specs=(placed, placed, placed, placed, P(), P(), P("dp", None, None)),
        out_specs=(placed, placed, placed, P(), P()),
        check_vma=False,
    )
```

```python
import jax
import jax.numpy as jnp
from jax import lax
from jax.experimental import pallas as pl
from jax.experimental.pallas import tpu as pltpu
from jax.sharding import PartitionSpec as P


HD = 128
TILE = 64
ROWS = 16
FAR = -(1 << 20)
GROUP = 4
SIDE = 4

epsilon = 1e-06


def cost(flops, moved, exps=0):
    return pl.CostEstimate(flops=flops, bytes_accessed=moved, transcendentals=exps)


def room(mebibytes):
    return pltpu.CompilerParams(vmem_limit_bytes=mebibytes << 20)


def in_hbm(block):
    return pltpu.with_memory_space_constraint(block, pltpu.HBM)


def plan_kernel(listed_ref, plan_ref, slot_ref, *, blocks, listed):
    count = blocks * listed

    def bits(start):
        def step(i, mask):
            tile = listed_ref[start + i]
            inside = jnp.logical_and(tile >= -blocks, tile < 2 * blocks)
            bit = lax.shift_left(jnp.int32(1), jnp.where(inside, tile + blocks, 0))
            return mask | jnp.where(inside, bit, 0)

        return lax.fori_loop(0, count, step, jnp.int32(0))

    before, own, after = bits(0), bits(count), bits(2 * count)
    for i in range(16):
        plan_ref[count + i] = 0
    plan_ref[count + 7] = listed_ref[3 * count]
    low, high, to_after, to_before = (jnp.int32(0),) * 4
    for b in range(blocks):
        slot_ref[b] = blocks + low
        slot_ref[blocks + b] = jnp.int32(b)
        slot_ref[2 * blocks + b] = blocks + SIDE + high
        low += lax.shift_right_logical(own, jnp.int32(b)) & 1
        high += lax.shift_right_logical(own, jnp.int32(2 * blocks + b)) & 1
        plan_ref[count + to_after] = jnp.int32(b)
        to_after += lax.shift_right_logical(after, jnp.int32(blocks + b)) & 1
        plan_ref[count + 8 + to_before] = jnp.int32(b)
        to_before += lax.shift_right_logical(before, jnp.int32(blocks + b)) & 1

    def place(i, carry):
        tile = jnp.clip(listed_ref[count + i], -blocks, 2 * blocks - 1)
        plan_ref[i] = slot_ref[tile + blocks]
        return carry

    lax.fori_loop(0, count, place, jnp.int32(0))


def make_plan(key_tiles, blocks):
    listed = key_tiles.shape[2]
    start = lax.axis_index("ctx") * blocks
    padded = jnp.pad(key_tiles[0] - start, ((blocks, blocks), (0, 0)), constant_values=FAR)
    near = lax.dynamic_slice_in_dim(padded, start, 3 * blocks, 0).reshape(-1)
    near = jnp.append(near, lax.axis_index("head"))
    count = blocks * listed
    return pl.pallas_call(
        lambda a, b, c: plan_kernel(a, b, c, blocks=blocks, listed=listed),
        out_shape=jax.ShapeDtypeStruct((count + 16,), jnp.int32),
        in_specs=[pl.BlockSpec(memory_space=pltpu.SMEM)],
        out_specs=pl.BlockSpec(memory_space=pltpu.SMEM),
        scratch_shapes=[pltpu.SMEM((3 * blocks,), jnp.int32)],
        cost_estimate=cost(1000, 1000),
        name="plan",
    )(near)


def norm_kernel(x_ref, y_ref, gain_ref, out_ref, *, groups, heads):
    width = groups * heads * HD

    def step(c, carry):
        rows = pl.ds(c * ROWS, ROWS)
        x = x_ref[rows, :].astype(jnp.float32)
        scaling = lax.rsqrt(jnp.sum(x * x, axis=-1, keepdims=True) / width + epsilon)
        for g in range(groups):
            for h in range(heads):
                cols = slice((g * heads + h) * HD, (g * heads + h + 1) * HD)
                part = x_ref[rows, cols].astype(jnp.float32) * scaling * gain_ref[cols][None, :]
                out_ref[g, 0, h, 0, rows, :] = part.astype(jnp.bfloat16)
                out_ref[g, 1, h, 0, rows, :] = y_ref[rows, cols]
        return carry

    lax.fori_loop(0, TILE // ROWS, step, 0)


def norm_pack(x, y, gain, groups, grant):
    tokens, width = x.shape
    heads = width // HD // groups
    tiles = tokens // TILE
    return pl.pallas_call(
        lambda *refs: norm_kernel(*refs, groups=groups, heads=heads),
        grid=(tiles,),
        out_shape=jax.ShapeDtypeStruct((groups, 2, heads, tiles, TILE, HD), jnp.bfloat16),
        in_specs=[
            pl.BlockSpec((TILE, width), lambda i: (i, 0)),
            pl.BlockSpec((TILE, width), lambda i: (i, 0)),
            pl.BlockSpec((width,), lambda i: (0,)),
        ],
        out_specs=pl.BlockSpec(
            (groups, 2, heads, 1, TILE, HD), lambda i: (0, 0, 0, i, 0, 0)
        ),
        compiler_params=room(grant),
        cost_estimate=cost(8 * tokens * width, 8 * tokens * width),
    )(x, y, gain)


def norm_turned_kernel(plan_ref, x_ref, y_ref, gain_ref, *outs, count, heads):
    groups = len(outs)
    width = groups * heads * HD
    me = plan_ref[count + 7]

    def step(c, carry):
        rows = pl.ds(c * ROWS, ROWS)
        x = x_ref[rows, :].astype(jnp.float32)
        scaling = lax.rsqrt(jnp.sum(x * x, axis=-1, keepdims=True) / width + epsilon)
        for s, out_ref in enumerate(outs):
            start = lax.rem(me + s, groups) * (heads * HD)
            for h in range(heads):
                cols = pl.ds(pl.multiple_of(start + h * HD, HD), HD)
                part = x_ref[rows, cols].astype(jnp.float32) * scaling * gain_ref[cols][None, :]
                out_ref[0, h, 0, rows, :] = part.astype(jnp.bfloat16)
                out_ref[1, h, 0, rows, :] = y_ref[rows, cols]
        return carry

    lax.fori_loop(0, TILE // ROWS, step, 0)


def norm_turned(plan, x, y, gain, groups, count):
    tokens, width = x.shape
    heads = width // HD // groups
    tiles = tokens // TILE
    rows = pl.BlockSpec((TILE, width), lambda i: (i, 0))
    return pl.pallas_call(
        lambda *refs: norm_turned_kernel(*refs, count=count, heads=heads),
        grid=(tiles,),
        out_shape=[jax.ShapeDtypeStruct((2, heads, tiles, TILE, HD), jnp.bfloat16)] * groups,
        in_specs=[
            pl.BlockSpec(memory_space=pltpu.SMEM),
            rows,
            rows,
            pl.BlockSpec((width,), lambda i: (0,)),
        ],
        out_specs=[pl.BlockSpec((2, heads, 1, TILE, HD), lambda i: (0, 0, i, 0, 0))] * groups,
        compiler_params=room(16),
        cost_estimate=cost(8 * tokens * width, 8 * tokens * width),
        name="norm_query",
    )(plan, x, y, gain)


def unnorm_kernel(xq_ref, xk_ref, back_ref, gq_ref, gk_ref, oq_ref, ok_ref, ov_ref, *, groups, heads):
    width = groups * heads * HD
    places = [(g, h, slice((g * heads + h) * HD, (g * heads + h + 1) * HD)) for g in range(groups) for h in range(heads)]

    def step(c, carry):
        rows = pl.ds(c * ROWS, ROWS)
        for which, x_ref, gain_ref, out_ref in ((0, xq_ref, gq_ref, oq_ref), (1, xk_ref, gk_ref, ok_ref)):
            square = jnp.zeros((ROWS, HD), jnp.float32)
            total = jnp.zeros((ROWS, HD), jnp.float32)
            for g, h, cols in places:
                x = x_ref[rows, cols].astype(jnp.float32)
                gained = back_ref[g, which, h, 0, rows, :].astype(jnp.float32) * gain_ref[cols][None, :]
                square += x * x
                total += gained * x
            scaling = lax.rsqrt(jnp.sum(square, axis=-1, keepdims=True) / width + epsilon)
            mean = jnp.sum(total, axis=-1, keepdims=True) / width
            factor = scaling * scaling * scaling * mean
            for g, h, cols in places:
                x = x_ref[rows, cols].astype(jnp.float32)
                gained = back_ref[g, which, h, 0, rows, :].astype(jnp.float32) * gain_ref[cols][None, :]
                out_ref[rows, cols] = (scaling * gained - x * factor).astype(jnp.bfloat16)
                if which:
                    ov_ref[rows, cols] = back_ref[g, 2, h, 0, rows, :]
        return carry

    lax.fori_loop(0, TILE // ROWS, step, 0)


def unnorm(xq, xk, back, gain_query, gain_key):
    tokens, width = xq.shape
    groups, _, heads = back.shape[:3]
    rows = pl.BlockSpec((TILE, width), lambda i: (i, 0))
    gain = pl.BlockSpec((width,), lambda i: (0,))
    return pl.pallas_call(
        lambda *refs: unnorm_kernel(*refs, groups=groups, heads=heads),
        grid=(tokens // TILE,),
        out_shape=[jax.ShapeDtypeStruct((tokens, width), jnp.bfloat16)] * 3,
        in_specs=[
            rows,
            rows,
            pl.BlockSpec((groups, 3, heads, 1, TILE, HD), lambda i: (0, 0, 0, i, 0, 0)),
            gain,
            gain,
        ],
        out_specs=[rows] * 3,
        compiler_params=room(16),
        cost_estimate=cost(24 * tokens * width, 16 * tokens * width),
        name="unnorm",
    )(xq, xk, back, gain_query, gain_key)


def pack_kernel(plan_ref, kv_ref, after_ref, before_ref, *, count):
    for which, out_ref in ((0, after_ref), (8, before_ref)):
        for r in range(SIDE):
            tile = plan_ref[count + which + r]
            for kv in range(2):
                out_ref[kv, 0, r] = kv_ref[tile // 2, kv, 0, tile % 2]


def pack(plan, kv, count):
    groups, _, heads, tiles, _, _ = kv.shape
    side = jax.ShapeDtypeStruct((2, heads, SIDE, TILE, HD), kv.dtype)
    side_spec = pl.BlockSpec((2, 1, SIDE, TILE, HD), lambda h: (0, h, 0, 0, 0))
    return pl.pallas_call(
        lambda *refs: pack_kernel(*refs, count=count),
        grid=(heads,),
        out_shape=[side, side],
        in_specs=[
            pl.BlockSpec(memory_space=pltpu.SMEM),
            pl.BlockSpec((groups, 2, 1, tiles, TILE, HD), lambda h: (0, 0, h, 0, 0, 0)),
        ],
        out_specs=[side_spec, side_spec],
        compiler_params=room(8),
        cost_estimate=cost(1000, 4 * kv.size),
        name="pack",
    )(plan, kv)


def merge_kernel(plan_ref, dq_ref, own_ref, after_ref, before_ref, out_ref, total_ref, *, count):
    total_ref[...] = own_ref[:, :, 0].astype(jnp.float32)
    for which, side_ref in ((0, after_ref), (8, before_ref)):
        for r in range(SIDE):
            tile = plan_ref[count + which + r]
            for kv in range(2):
                total_ref[tile // 2, kv, tile % 2] += side_ref[kv, 0, r].astype(jnp.float32)
    out_ref[:, 0, 0] = dq_ref[:, 0]
    out_ref[:, 1:, 0] = total_ref[...].astype(jnp.bfloat16)


def merge(plan, dq, own, after, before, count):
    groups, _, heads, tiles, _, _ = own.shape
    side_spec = pl.BlockSpec((2, 1, SIDE, TILE, HD), lambda h: (0, h, 0, 0, 0))
    return pl.pallas_call(
        lambda *refs: merge_kernel(*refs, count=count),
        grid=(heads,),
        out_shape=jax.ShapeDtypeStruct((groups, 3, heads, tiles, TILE, HD), jnp.bfloat16),
        in_specs=[
            pl.BlockSpec(memory_space=pltpu.SMEM),
            pl.BlockSpec((groups, 1, tiles, TILE, HD), lambda h: (0, h, 0, 0, 0)),
            pl.BlockSpec((groups, 2, 1, tiles, TILE, HD), lambda h: (0, 0, h, 0, 0, 0)),
            side_spec,
            side_spec,
        ],
        out_specs=pl.BlockSpec((groups, 3, 1, tiles, TILE, HD), lambda h: (0, 0, h, 0, 0, 0)),
        scratch_shapes=[pltpu.VMEM((groups, 2, tiles, TILE, HD), jnp.float32)],
        compiler_params=room(8),
        cost_estimate=cost(own.size, 6 * own.size),
        name="merge",
    )(plan, dq, own, after, before)


def dot(a, b, dims):
    return lax.dot_general(a, b, (dims, ((), ())), preferred_element_type=jnp.float32)


def attend_kernel(
    plan_ref,
    kv_ref,
    low_ref,
    high_ref,
    *refs,
    blocks,
    listed,
):
    qd_refs, refs = refs[: blocks // 2], refs[blocks // 2 :]
    dq_ref, own_ref, to_low_ref, to_high_ref, gain_ref, keys_ref, values_ref, dk_ref, dv_ref = refs
    groups = len(qd_refs)
    me = plan_ref[blocks * listed + 7]
    scaling = HD**-0.5
    slots = blocks + 2 * SIDE
    for b in range(blocks):
        keys_ref[b] = kv_ref[b // 2, 0, 0, b % 2]
        values_ref[b] = kv_ref[b // 2, 1, 0, b % 2]
    for r in range(SIDE):
        keys_ref[blocks + r] = low_ref[0, 0, r]
        values_ref[blocks + r] = low_ref[1, 0, r]
        keys_ref[blocks + SIDE + r] = high_ref[0, 0, r]
        values_ref[blocks + SIDE + r] = high_ref[1, 0, r]

    @pl.when(pl.program_id(0) == 0)
    def _():
        gain_ref[...] = jnp.zeros_like(gain_ref)

    dk_ref[...] = jnp.zeros_like(dk_ref)
    dv_ref[...] = jnp.zeros_like(dv_ref)

    def together(first, gain_sum):
        tiles = range(GROUP)
        far = [((first + t) // 2, (first + t) % 2) for t in tiles]
        where = [(lax.rem(me - s + groups, groups), half) for s, half in far]
        at = [
            [plan_ref[(2 * source + half) * listed + j] for j in range(listed)]
            for source, half in where
        ]
        queries = [qd_refs[s][0, 0, half] for s, half in far]
        gradient = [qd_refs[s][1, 0, half] for s, half in far]
        keys = [jnp.concatenate([keys_ref[a] for a in at[t]], axis=0) for t in tiles]
        vals = [jnp.concatenate([values_ref[a] for a in at[t]], axis=0) for t in tiles]
        scores = [dot(keys[t], queries[t], ((1,), (1,))) for t in tiles]
        dprob = [dot(vals[t], gradient[t], ((1,), (1,))) for t in tiles]
        largest = [jnp.max(x, axis=0, keepdims=True) for x in scores]
        powers = [jnp.exp((scores[t] - largest[t]) * scaling) for t in tiles]
        inverse = [1.0 / jnp.sum(x, axis=0, keepdims=True) for x in powers]
        weights = [powers[t] * inverse[t] for t in tiles]
        rounded = [x.astype(jnp.bfloat16) for x in weights]
        grad_value = [dot(rounded[t], gradient[t], ((1,), (0,))) for t in tiles]
        delta = [
            jnp.sum(rounded[t].astype(jnp.float32) * dprob[t], axis=0, keepdims=True)
            for t in tiles
        ]
        dscore = [(weights[t] * (dprob[t] - delta[t])).astype(jnp.bfloat16) for t in tiles]
        grad_key = [dot(dscore[t], queries[t], ((1,), (0,))) for t in tiles]
        grad_query = [
            (dot(dscore[t], keys[t], ((0,), (0,))) * scaling).astype(jnp.bfloat16) for t in tiles
        ]
        for t in tiles:
            dq_ref[where[t][0], 0, where[t][1]] = grad_query[t]
            product = grad_query[t].astype(jnp.float32) * queries[t].astype(jnp.float32)
            gain_sum += jnp.sum(product.reshape(-1, 8, HD), axis=0)
            for j, a in enumerate(at[t]):
                dk_ref[a] += grad_key[t][j * TILE : (j + 1) * TILE]
                dv_ref[a] += grad_value[t][j * TILE : (j + 1) * TILE]
        return gain_sum

    gain_query = jnp.zeros((8, HD), jnp.float32)
    for first in range(0, blocks, GROUP):
        gain_query = together(first, gain_query)
    gain_key = jnp.zeros((8, HD), jnp.float32)
    for s in range(slots):
        grad_key = dk_ref[s] * scaling
        gain_key += jnp.sum(
            (grad_key * keys_ref[s].astype(jnp.float32)).reshape(-1, 8, HD), axis=0
        )
        if s < blocks:
            own_ref[s // 2, 0, 0, s % 2] = grad_key.astype(jnp.bfloat16)
            own_ref[s // 2, 1, 0, s % 2] = dv_ref[s].astype(jnp.bfloat16)
        else:
            out_ref = to_low_ref if s < blocks + SIDE else to_high_ref
            r = (s - blocks) % SIDE
            out_ref[0, 0, r] = grad_key.astype(jnp.bfloat16)
            out_ref[1, 0, r] = dv_ref[s].astype(jnp.bfloat16)
    head = pl.program_id(0)
    for which, part in ((0, gain_query), (8, gain_key)):
        gain_ref[pl.ds(which + head, 1)] = jnp.sum(part, axis=0, keepdims=True)


def attend(plan, qd, kv, low, high, blocks, listed):
    groups, _, heads, tiles, _, _ = kv.shape
    slots = blocks + 2 * SIDE
    side = jax.ShapeDtypeStruct(low.shape, jnp.bfloat16)
    side_spec = pl.BlockSpec((2, 1, SIDE, TILE, HD), lambda h: (0, h, 0, 0, 0))
    block = pl.BlockSpec((groups, 2, 1, tiles, TILE, HD), lambda h: (0, 0, h, 0, 0, 0))
    work = heads * blocks * TILE * listed * TILE
    return pl.pallas_call(
        lambda *refs: attend_kernel(*refs, blocks=blocks, listed=listed),
        grid=(heads,),
        out_shape=[
            jax.ShapeDtypeStruct((groups, heads, tiles, TILE, HD), jnp.bfloat16),
            pltpu.HBM(kv.shape, jnp.bfloat16),
            side,
            side,
            jax.ShapeDtypeStruct((16, HD), jnp.float32),
        ],
        in_specs=[pl.BlockSpec(memory_space=pltpu.SMEM), block, side_spec, side_spec]
        + [pl.BlockSpec((2, 1, tiles, TILE, HD), lambda h: (0, h, 0, 0, 0))] * groups,
        out_specs=[
            pl.BlockSpec((groups, 1, tiles, TILE, HD), lambda h: (0, h, 0, 0, 0)),
            block,
            side_spec,
            side_spec,
            pl.BlockSpec((16, HD), lambda h: (0, 0)),
        ],
        scratch_shapes=[
            pltpu.VMEM((slots, TILE, HD), jnp.bfloat16),
            pltpu.VMEM((slots, TILE, HD), jnp.bfloat16),
            pltpu.VMEM((slots, TILE, HD), jnp.float32),
            pltpu.VMEM((slots, TILE, HD), jnp.float32),
        ],
        compiler_params=room(24),
        cost_estimate=cost(12 * work * HD, 20 * kv.size, work),
        name="attend",
    )(plan, kv, low, high, *qd)


def swap(block):
    return lax.all_to_all(block, "head", split_axis=0, concat_axis=0, tiled=True)


def shift(block, distance):
    devices = range(lax.axis_size("ctx"))
    route = [(i - distance, i) for i in devices if i - distance in devices]
    return lax.ppermute(block, "ctx", route)


def turn(block, distance):
    count = lax.axis_size("head")
    return lax.ppermute(block, "head", [(i, (i + distance) % count) for i in range(count)])


def gathered(block, axis):
    count = lax.axis_size(axis)
    copies = jnp.broadcast_to(block[None], (count,) + block.shape)
    return lax.all_to_all(copies, axis, split_axis=0, concat_axis=0, tiled=True)


def per_device(x_query, x_key, values, grad_out, gain_query, gain_key, key_tiles):
    groups = lax.axis_size("head")
    blocks = groups * x_query.shape[1] // TILE
    listed = key_tiles.shape[2]
    count = blocks * listed
    kv = norm_pack(x_key[0], values[0], gain_key, groups, 60)
    kv = swap(kv)
    plan = make_plan(key_tiles, blocks)
    qd = norm_turned(plan, x_query[0], grad_out[0], gain_query, groups, count)
    qd = [qd[0]] + [turn(qd[s], s) for s in range(1, groups)]
    after, before = pack(plan, kv, count)
    low, high = shift(after, 1), shift(before, -1)
    low, high = in_hbm(low), in_hbm(high)
    dq, own, to_low, to_high, gains = attend(plan, qd, kv, low, high, blocks, listed)
    from_after, from_before = shift(to_low, -1), shift(to_high, 1)
    gains = jnp.sum(gathered(gains, "dp"), axis=0)
    from_after, from_before, gains = lax.optimization_barrier((from_after, from_before, gains))
    merged = merge(plan, dq, own, from_after, from_before, count)
    merged, gains = lax.optimization_barrier((merged, gains))
    back = swap(merged)
    gains = jnp.sum(lax.all_gather(gains, "ctx"), axis=0)
    gains = lax.all_gather(gains, "head")
    grad_x_query, grad_x_key, grad_values = unnorm(
        x_query[0], x_key[0], back, gain_query, gain_key
    )
    heads = x_query.shape[2] // HD // groups
    gains = [gains[:, at : at + heads].reshape(-1) for at in (0, 8)]
    samples = lax.axis_size("dp")
    return (
        grad_x_query[None],
        grad_x_key[None],
        grad_values[None],
        gains[0] / gain_query / samples,
        gains[1] / gain_key / samples,
    )


def solution(mesh):
    placed = P("dp", ("ctx", "head"), None)
    return jax.shard_map(
        per_device,
        mesh=mesh,
        in_specs=(placed, placed, placed, placed, P(), P(), P("dp", None, None)),
        out_specs=(placed, placed, placed, P(), P()),
        check_vma=False,
    )
```

```python
import jax
import jax.numpy as jnp
from jax import lax
from jax.experimental import pallas as pl
from jax.experimental.pallas import tpu as pltpu
from jax.sharding import PartitionSpec as P


HD = 128
TILE = 64
ROWS = 16
FAR = -(1 << 20)
GROUP = 4
SIDE = 4

epsilon = 1e-06


def cost(flops, moved, exps=0):
    return pl.CostEstimate(flops=flops, bytes_accessed=moved, transcendentals=exps)


def room(mebibytes):
    return pltpu.CompilerParams(vmem_limit_bytes=mebibytes << 20)


def in_hbm(block):
    return pltpu.with_memory_space_constraint(block, pltpu.HBM)


def plan_kernel(listed_ref, plan_ref, slot_ref, *, blocks, listed):
    count = blocks * listed

    def bits(start):
        def step(i, mask):
            tile = listed_ref[start + i]
            inside = jnp.logical_and(tile >= -blocks, tile < 2 * blocks)
            bit = lax.shift_left(jnp.int32(1), jnp.where(inside, tile + blocks, 0))
            return mask | jnp.where(inside, bit, 0)

        return lax.fori_loop(0, count, step, jnp.int32(0))

    before, own, after = bits(0), bits(count), bits(2 * count)
    for i in range(16):
        plan_ref[count + i] = 0
    plan_ref[count + 7] = listed_ref[3 * count]
    low, high, to_after, to_before = (jnp.int32(0),) * 4
    for b in range(blocks):
        slot_ref[b] = blocks + low
        slot_ref[blocks + b] = jnp.int32(b)
        slot_ref[2 * blocks + b] = blocks + SIDE + high
        low += lax.shift_right_logical(own, jnp.int32(b)) & 1
        high += lax.shift_right_logical(own, jnp.int32(2 * blocks + b)) & 1
        plan_ref[count + to_after] = jnp.int32(b)
        to_after += lax.shift_right_logical(after, jnp.int32(blocks + b)) & 1
        plan_ref[count + 8 + to_before] = jnp.int32(b)
        to_before += lax.shift_right_logical(before, jnp.int32(blocks + b)) & 1

    def place(i, carry):
        tile = jnp.clip(listed_ref[count + i], -blocks, 2 * blocks - 1)
        plan_ref[i] = slot_ref[tile + blocks]
        return carry

    lax.fori_loop(0, count, place, jnp.int32(0))


def make_plan(key_tiles, blocks):
    listed = key_tiles.shape[2]
    start = lax.axis_index("ctx") * blocks
    padded = jnp.pad(key_tiles[0] - start, ((blocks, blocks), (0, 0)), constant_values=FAR)
    near = lax.dynamic_slice_in_dim(padded, start, 3 * blocks, 0).reshape(-1)
    near = jnp.append(near, lax.axis_index("head"))
    count = blocks * listed
    return pl.pallas_call(
        lambda a, b, c: plan_kernel(a, b, c, blocks=blocks, listed=listed),
        out_shape=jax.ShapeDtypeStruct((count + 16,), jnp.int32),
        in_specs=[pl.BlockSpec(memory_space=pltpu.SMEM)],
        out_specs=pl.BlockSpec(memory_space=pltpu.SMEM),
        scratch_shapes=[pltpu.SMEM((3 * blocks,), jnp.int32)],
        cost_estimate=cost(1000, 1000),
        name="plan",
    )(near)


def norm_kernel(x_ref, y_ref, gain_ref, out_ref, *, groups, heads):
    width = groups * heads * HD

    def step(c, carry):
        rows = pl.ds(c * ROWS, ROWS)
        x = x_ref[rows, :].astype(jnp.float32)
        scaling = lax.rsqrt(jnp.sum(x * x, axis=-1, keepdims=True) / width + epsilon)
        for g in range(groups):
            for h in range(heads):
                cols = slice((g * heads + h) * HD, (g * heads + h + 1) * HD)
                part = x_ref[rows, cols].astype(jnp.float32) * scaling * gain_ref[cols][None, :]
                out_ref[g, 0, h, 0, rows, :] = part.astype(jnp.bfloat16)
                out_ref[g, 1, h, 0, rows, :] = y_ref[rows, cols]
        return carry

    lax.fori_loop(0, TILE // ROWS, step, 0)


def norm_pack(x, y, gain, groups, grant):
    tokens, width = x.shape
    heads = width // HD // groups
    tiles = tokens // TILE
    return pl.pallas_call(
        lambda *refs: norm_kernel(*refs, groups=groups, heads=heads),
        grid=(tiles,),
        out_shape=jax.ShapeDtypeStruct((groups, 2, heads, tiles, TILE, HD), jnp.bfloat16),
        in_specs=[
            pl.BlockSpec((TILE, width), lambda i: (i, 0)),
            pl.BlockSpec((TILE, width), lambda i: (i, 0)),
            pl.BlockSpec((width,), lambda i: (0,)),
        ],
        out_specs=pl.BlockSpec(
            (groups, 2, heads, 1, TILE, HD), lambda i: (0, 0, 0, i, 0, 0)
        ),
        compiler_params=room(grant),
        cost_estimate=cost(8 * tokens * width, 8 * tokens * width),
    )(x, y, gain)


def norm_turned_kernel(plan_ref, x_ref, y_ref, gain_ref, *outs, count, heads):
    groups = len(outs)
    width = groups * heads * HD
    me = plan_ref[count + 7]

    def step(c, carry):
        rows = pl.ds(c * ROWS, ROWS)
        x = x_ref[rows, :].astype(jnp.float32)
        scaling = lax.rsqrt(jnp.sum(x * x, axis=-1, keepdims=True) / width + epsilon)
        for s, out_ref in enumerate(outs):
            start = lax.rem(me + s, groups) * (heads * HD)
            for h in range(heads):
                cols = pl.ds(pl.multiple_of(start + h * HD, HD), HD)
                part = x_ref[rows, cols].astype(jnp.float32) * scaling * gain_ref[cols][None, :]
                out_ref[0, h, 0, rows, :] = part.astype(jnp.bfloat16)
                out_ref[1, h, 0, rows, :] = y_ref[rows, cols]
        return carry

    lax.fori_loop(0, TILE // ROWS, step, 0)


def norm_turned(plan, x, y, gain, groups, count):
    tokens, width = x.shape
    heads = width // HD // groups
    tiles = tokens // TILE
    rows = pl.BlockSpec((TILE, width), lambda i: (i, 0))
    return pl.pallas_call(
        lambda *refs: norm_turned_kernel(*refs, count=count, heads=heads),
        grid=(tiles,),
        out_shape=[jax.ShapeDtypeStruct((2, heads, tiles, TILE, HD), jnp.bfloat16)] * groups,
        in_specs=[
            pl.BlockSpec(memory_space=pltpu.SMEM),
            rows,
            rows,
            pl.BlockSpec((width,), lambda i: (0,)),
        ],
        out_specs=[pl.BlockSpec((2, heads, 1, TILE, HD), lambda i: (0, 0, i, 0, 0))] * groups,
        compiler_params=room(16),
        cost_estimate=cost(8 * tokens * width, 8 * tokens * width),
        name="norm_query",
    )(plan, x, y, gain)


def unnorm_kernel(
    xq_ref,
    xk_ref,
    back_ref,
    gq_ref,
    gk_ref,
    sums_ref,
    oq_ref,
    ok_ref,
    ov_ref,
    sq_ref,
    sk_ref,
    *,
    groups,
    heads,
    samples,
):
    width = groups * heads * HD
    places = [(g, h, slice((g * heads + h) * HD, (g * heads + h + 1) * HD)) for g in range(groups) for h in range(heads)]

    def step(c, carry):
        rows = pl.ds(c * ROWS, ROWS)
        for which, x_ref, gain_ref, out_ref in ((0, xq_ref, gq_ref, oq_ref), (1, xk_ref, gk_ref, ok_ref)):
            square = jnp.zeros((ROWS, HD), jnp.float32)
            total = jnp.zeros((ROWS, HD), jnp.float32)
            for g, h, cols in places:
                x = x_ref[rows, cols].astype(jnp.float32)
                gained = back_ref[g, which, h, 0, rows, :].astype(jnp.float32) * gain_ref[cols][None, :]
                square += x * x
                total += gained * x
            scaling = lax.rsqrt(jnp.sum(square, axis=-1, keepdims=True) / width + epsilon)
            mean = jnp.sum(total, axis=-1, keepdims=True) / width
            factor = scaling * scaling * scaling * mean
            for g, h, cols in places:
                x = x_ref[rows, cols].astype(jnp.float32)
                gained = back_ref[g, which, h, 0, rows, :].astype(jnp.float32) * gain_ref[cols][None, :]
                out_ref[rows, cols] = (scaling * gained - x * factor).astype(jnp.bfloat16)
                if which:
                    ov_ref[rows, cols] = back_ref[g, 2, h, 0, rows, :]
        return carry

    lax.fori_loop(0, TILE // ROWS, step, 0)

    @pl.when(pl.program_id(0) == 0)
    def _():
        for row, gain_ref, out_ref in ((0, gq_ref, sq_ref), (8, gk_ref, sk_ref)):
            for g, h, cols in places:
                out_ref[cols] = sums_ref[g, row + h] / gain_ref[cols] / samples


def unnorm(xq, xk, back, gain_query, gain_key, sums, samples):
    tokens, width = xq.shape
    groups, _, heads = back.shape[:3]
    rows = pl.BlockSpec((TILE, width), lambda i: (i, 0))
    gain = pl.BlockSpec((width,), lambda i: (0,))
    total = jax.ShapeDtypeStruct((width,), jnp.float32)
    return pl.pallas_call(
        lambda *refs: unnorm_kernel(*refs, groups=groups, heads=heads, samples=samples),
        grid=(tokens // TILE,),
        out_shape=[jax.ShapeDtypeStruct((tokens, width), jnp.bfloat16)] * 3 + [total] * 2,
        in_specs=[
            rows,
            rows,
            pl.BlockSpec((groups, 3, heads, 1, TILE, HD), lambda i: (0, 0, 0, i, 0, 0)),
            gain,
            gain,
            pl.BlockSpec(sums.shape, lambda i: (0, 0, 0)),
        ],
        out_specs=[rows] * 3 + [gain] * 2,
        compiler_params=room(16),
        cost_estimate=cost(24 * tokens * width, 16 * tokens * width),
        name="unnorm",
    )(xq, xk, back, gain_query, gain_key, sums)


def pack_kernel(plan_ref, kv_ref, after_ref, before_ref, *, count):
    for which, out_ref in ((0, after_ref), (8, before_ref)):
        for r in range(SIDE):
            tile = plan_ref[count + which + r]
            for kv in range(2):
                out_ref[kv, 0, r] = kv_ref[tile // 2, kv, 0, tile % 2]


def pack(plan, kv, count):
    groups, _, heads, tiles, _, _ = kv.shape
    side = jax.ShapeDtypeStruct((2, heads, SIDE, TILE, HD), kv.dtype)
    side_spec = pl.BlockSpec((2, 1, SIDE, TILE, HD), lambda h: (0, h, 0, 0, 0))
    return pl.pallas_call(
        lambda *refs: pack_kernel(*refs, count=count),
        grid=(heads,),
        out_shape=[side, side],
        in_specs=[
            pl.BlockSpec(memory_space=pltpu.SMEM),
            pl.BlockSpec((groups, 2, 1, tiles, TILE, HD), lambda h: (0, 0, h, 0, 0, 0)),
        ],
        out_specs=[side_spec, side_spec],
        compiler_params=room(8),
        cost_estimate=cost(1000, 4 * kv.size),
        name="pack",
    )(plan, kv)


def merge_kernel(
    plan_ref,
    dq_ref,
    own_ref,
    after_ref,
    before_ref,
    parts_ref,
    out_ref,
    sum_ref,
    total_ref,
    *,
    count,
):
    @pl.when(pl.program_id(0) == 0)
    def _():
        sum_ref[...] = jnp.sum(parts_ref[...], axis=0)

    total_ref[...] = own_ref[:, :, 0].astype(jnp.float32)
    for which, side_ref in ((0, after_ref), (8, before_ref)):
        for r in range(SIDE):
            tile = plan_ref[count + which + r]
            for kv in range(2):
                total_ref[tile // 2, kv, tile % 2] += side_ref[kv, 0, r].astype(jnp.float32)
    out_ref[:, 0, 0] = dq_ref[:, 0]
    out_ref[:, 1:, 0] = total_ref[...].astype(jnp.bfloat16)


def merge(plan, dq, own, after, before, parts, count):
    groups, _, heads, tiles, _, _ = own.shape
    side_spec = pl.BlockSpec((2, 1, SIDE, TILE, HD), lambda h: (0, h, 0, 0, 0))
    return pl.pallas_call(
        lambda *refs: merge_kernel(*refs, count=count),
        grid=(heads,),
        out_shape=[
            pltpu.HBM((groups, 3, heads, tiles, TILE, HD), jnp.bfloat16),
            jax.ShapeDtypeStruct(parts.shape[1:], jnp.float32),
        ],
        in_specs=[
            pl.BlockSpec(memory_space=pltpu.SMEM),
            pl.BlockSpec((groups, 1, tiles, TILE, HD), lambda h: (0, h, 0, 0, 0)),
            pl.BlockSpec((groups, 2, 1, tiles, TILE, HD), lambda h: (0, 0, h, 0, 0, 0)),
            side_spec,
            side_spec,
            pl.BlockSpec(parts.shape, lambda h: (0, 0, 0)),
        ],
        out_specs=[
            pl.BlockSpec((groups, 3, 1, tiles, TILE, HD), lambda h: (0, 0, h, 0, 0, 0)),
            pl.BlockSpec(parts.shape[1:], lambda h: (0, 0)),
        ],
        scratch_shapes=[pltpu.VMEM((groups, 2, tiles, TILE, HD), jnp.float32)],
        compiler_params=room(8),
        cost_estimate=cost(own.size, 6 * own.size),
        name="merge",
    )(plan, dq, own, after, before, parts)


def dot(a, b, dims):
    return lax.dot_general(a, b, (dims, ((), ())), preferred_element_type=jnp.float32)


def attend_kernel(
    plan_ref,
    kv_ref,
    low_ref,
    high_ref,
    *refs,
    blocks,
    listed,
):
    qd_refs, refs = refs[: blocks // 2], refs[blocks // 2 :]
    dq_ref, own_ref, to_low_ref, to_high_ref, gain_ref, keys_ref, values_ref, dk_ref, dv_ref = refs
    groups = len(qd_refs)
    me = plan_ref[blocks * listed + 7]
    scaling = HD**-0.5
    slots = blocks + 2 * SIDE
    for b in range(blocks):
        keys_ref[b] = kv_ref[b // 2, 0, 0, b % 2]
        values_ref[b] = kv_ref[b // 2, 1, 0, b % 2]
    for r in range(SIDE):
        keys_ref[blocks + r] = low_ref[0, 0, r]
        values_ref[blocks + r] = low_ref[1, 0, r]
        keys_ref[blocks + SIDE + r] = high_ref[0, 0, r]
        values_ref[blocks + SIDE + r] = high_ref[1, 0, r]

    @pl.when(pl.program_id(0) == 0)
    def _():
        gain_ref[...] = jnp.zeros_like(gain_ref)

    dk_ref[...] = jnp.zeros_like(dk_ref)
    dv_ref[...] = jnp.zeros_like(dv_ref)

    def together(first, gain_sum):
        tiles = range(GROUP)
        far = [((first + t) // 2, (first + t) % 2) for t in tiles]
        where = [(lax.rem(me - s + groups, groups), half) for s, half in far]
        at = [
            [plan_ref[(2 * source + half) * listed + j] for j in range(listed)]
            for source, half in where
        ]
        queries = [qd_refs[s][0, 0, half] for s, half in far]
        gradient = [qd_refs[s][1, 0, half] for s, half in far]
        keys = [jnp.concatenate([keys_ref[a] for a in at[t]], axis=0) for t in tiles]
        vals = [jnp.concatenate([values_ref[a] for a in at[t]], axis=0) for t in tiles]
        scores = [dot(keys[t], queries[t], ((1,), (1,))) for t in tiles]
        dprob = [dot(vals[t], gradient[t], ((1,), (1,))) for t in tiles]
        largest = [jnp.max(x, axis=0, keepdims=True) for x in scores]
        powers = [jnp.exp((scores[t] - largest[t]) * scaling) for t in tiles]
        inverse = [1.0 / jnp.sum(x, axis=0, keepdims=True) for x in powers]
        weights = [powers[t] * inverse[t] for t in tiles]
        rounded = [x.astype(jnp.bfloat16) for x in weights]
        grad_value = [dot(rounded[t], gradient[t], ((1,), (0,))) for t in tiles]
        delta = [
            jnp.sum(rounded[t].astype(jnp.float32) * dprob[t], axis=0, keepdims=True)
            for t in tiles
        ]
        dscore = [(weights[t] * (dprob[t] - delta[t])).astype(jnp.bfloat16) for t in tiles]
        grad_key = [dot(dscore[t], queries[t], ((1,), (0,))) for t in tiles]
        grad_query = [
            (dot(dscore[t], keys[t], ((0,), (0,))) * scaling).astype(jnp.bfloat16) for t in tiles
        ]
        for t in tiles:
            dq_ref[where[t][0], 0, where[t][1]] = grad_query[t]
            product = grad_query[t].astype(jnp.float32) * queries[t].astype(jnp.float32)
            gain_sum += jnp.sum(product.reshape(-1, 8, HD), axis=0)
            for j, a in enumerate(at[t]):
                dk_ref[a] += grad_key[t][j * TILE : (j + 1) * TILE]
                dv_ref[a] += grad_value[t][j * TILE : (j + 1) * TILE]
        return gain_sum

    gain_query = jnp.zeros((8, HD), jnp.float32)
    for first in range(0, blocks, GROUP):
        gain_query = together(first, gain_query)
    gain_key = jnp.zeros((8, HD), jnp.float32)
    for s in range(slots):
        grad_key = dk_ref[s] * scaling
        gain_key += jnp.sum(
            (grad_key * keys_ref[s].astype(jnp.float32)).reshape(-1, 8, HD), axis=0
        )
        if s < blocks:
            own_ref[s // 2, 0, 0, s % 2] = grad_key.astype(jnp.bfloat16)
            own_ref[s // 2, 1, 0, s % 2] = dv_ref[s].astype(jnp.bfloat16)
        else:
            out_ref = to_low_ref if s < blocks + SIDE else to_high_ref
            r = (s - blocks) % SIDE
            out_ref[0, 0, r] = grad_key.astype(jnp.bfloat16)
            out_ref[1, 0, r] = dv_ref[s].astype(jnp.bfloat16)
    head = pl.program_id(0)
    for which, part in ((0, gain_query), (8, gain_key)):
        row = jnp.sum(part, axis=0, keepdims=True)
        for copy in range(gain_ref.shape[0]):
            gain_ref[copy, pl.ds(which + head, 1)] = row


def attend(plan, qd, kv, low, high, blocks, listed, copies):
    groups, _, heads, tiles, _, _ = kv.shape
    slots = blocks + 2 * SIDE
    side = jax.ShapeDtypeStruct(low.shape, jnp.bfloat16)
    side_spec = pl.BlockSpec((2, 1, SIDE, TILE, HD), lambda h: (0, h, 0, 0, 0))
    block = pl.BlockSpec((groups, 2, 1, tiles, TILE, HD), lambda h: (0, 0, h, 0, 0, 0))
    work = heads * blocks * TILE * listed * TILE
    return pl.pallas_call(
        lambda *refs: attend_kernel(*refs, blocks=blocks, listed=listed),
        grid=(heads,),
        out_shape=[
            jax.ShapeDtypeStruct((groups, heads, tiles, TILE, HD), jnp.bfloat16),
            pltpu.HBM(kv.shape, jnp.bfloat16),
            side,
            side,
            jax.ShapeDtypeStruct((copies, 16, HD), jnp.float32),
        ],
        in_specs=[pl.BlockSpec(memory_space=pltpu.SMEM), block, side_spec, side_spec]
        + [pl.BlockSpec((2, 1, tiles, TILE, HD), lambda h: (0, h, 0, 0, 0))] * groups,
        out_specs=[
            pl.BlockSpec((groups, 1, tiles, TILE, HD), lambda h: (0, h, 0, 0, 0)),
            block,
            side_spec,
            side_spec,
            pl.BlockSpec((copies, 16, HD), lambda h: (0, 0, 0)),
        ],
        scratch_shapes=[
            pltpu.VMEM((slots, TILE, HD), jnp.bfloat16),
            pltpu.VMEM((slots, TILE, HD), jnp.bfloat16),
            pltpu.VMEM((slots, TILE, HD), jnp.float32),
            pltpu.VMEM((slots, TILE, HD), jnp.float32),
        ],
        compiler_params=room(24),
        cost_estimate=cost(12 * work * HD, 20 * kv.size, work),
        name="attend",
    )(plan, kv, low, high, *qd)


def swap(block):
    return lax.all_to_all(block, "head", split_axis=0, concat_axis=0, tiled=True)


def shift(block, distance):
    devices = range(lax.axis_size("ctx"))
    route = [(i - distance, i) for i in devices if i - distance in devices]
    return lax.ppermute(block, "ctx", route)


def turn(block, distance):
    count = lax.axis_size("head")
    return lax.ppermute(block, "head", [(i, (i + distance) % count) for i in range(count)])


def per_device(x_query, x_key, values, grad_out, gain_query, gain_key, key_tiles):
    groups = lax.axis_size("head")
    blocks = groups * x_query.shape[1] // TILE
    listed = key_tiles.shape[2]
    count = blocks * listed
    kv = norm_pack(x_key[0], values[0], gain_key, groups, 60)
    kv = swap(kv)
    plan = make_plan(key_tiles, blocks)
    qd = norm_turned(plan, x_query[0], grad_out[0], gain_query, groups, count)
    qd = [qd[0]] + [turn(qd[s], s) for s in range(1, groups)]
    after, before = pack(plan, kv, count)
    low, high = shift(after, 1), shift(before, -1)
    low, high = in_hbm(low), in_hbm(high)
    dq, own, to_low, to_high, gains = attend(
        plan, qd, kv, low, high, blocks, listed, lax.axis_size("dp")
    )
    from_after, from_before = shift(to_low, -1), shift(to_high, 1)
    gains = lax.all_to_all(gains, "dp", split_axis=0, concat_axis=0, tiled=True)
    from_after, from_before, gains = lax.optimization_barrier((from_after, from_before, gains))
    merged, gains = merge(plan, dq, in_hbm(own), from_after, from_before, gains, count)
    back = swap(merged)
    gains = jnp.sum(lax.all_gather(gains, "ctx"), axis=0)
    gains = lax.all_gather(gains, "head")
    grad_x_query, grad_x_key, grad_values, sum_query, sum_key = unnorm(
        x_query[0], x_key[0], back, gain_query, gain_key, gains, lax.axis_size("dp")
    )
    return grad_x_query[None], grad_x_key[None], grad_values[None], sum_query, sum_key


def solution(mesh):
    placed = P("dp", ("ctx", "head"), None)
    return jax.shard_map(
        per_device,
        mesh=mesh,
        in_specs=(placed, placed, placed, placed, P(), P(), P("dp", None, None)),
        out_specs=(placed, placed, placed, P(), P()),
        check_vma=False,
    )
```
